256 devices in a mesh: ctx: 32 (over x, z), tp: 8 (over y, core).
Axes of the slice: x: 4, y: 4, z: 8, core: 2. Of those that a mesh axis runs over, the one named last changes fastest.
Arguments:
- tokens: bfloat16 [16384, 4096], P('ctx', 'tp'), may hold values from -16 to 16
- query_weight: bfloat16 [4096, 4096], P(None, 'tp'), may hold values from -0.09375 to 0.09375
- key_weight: bfloat16 [4096, 1024], P(None, 'tp'), may hold values from -0.09375 to 0.09375
- value_weight: bfloat16 [4096, 1024], P(None, 'tp'), may hold values from -0.09375 to 0.09375
- out_weight: bfloat16 [4096, 4096], P('tp'), may hold values from -0.09375 to 0.09375
- links: int32 [128, 16], P('ctx'), may hold values from 0 to 127, as said below
- counts: int32 [128], P('ctx'), may hold values from 1 to 16, as said below
- doc_ids: int32 [128], replicated, may hold values from 0 to 31, never falling along the last dimension, each value on 1 to 8 neighbouring positions
Outputs:
- mixed: bfloat16 [16384, 4096], P(('ctx', 'tp'))
The draws below stay inside these ranges and needn't reach their ends.
Inputs may be any that keep to these rules, and one draw needn't show every extreme that they name: `links`: the first entry of each row is the query block itself; the entries of a row are distinct; every listed block lies within 4 ctx indices of its query block (block index // 4), and some query block of every ctx index lists a block exactly 4 indices away. `counts`: the first query block of each ctx index has 2 or more live slots, and block 0 has 16.
All inputs are finite; a program needn't handle non-finite values.
Results may differ from the reference program's by a relative error of at most 0.017.
Values may be sent and summed in bfloat16 or wider, within the bound.
No kernel may reach another device: no remote copies, remote signals or barrier semaphores. Data moves between devices by JAX's collectives and lax.ppermute only.
A program may use at most 64 MiB of HBM per device.

```python
import math
import jax
import jax.numpy as jnp
import numpy as np
from jax import lax

D = 4096
HEADS = 32
KV_HEADS = 8
HEAD_DIM = 128
BLOCK = 128
LINKS = 16
REACH = 4
SEQ = 16384
NBLK = 128
BLK_DEV = 4
DOCS = 32
N_TP = 8


def draw_tokens(key, part):
    first = jax.random.fold_in(key, 0)
    base = jax.random.normal(first, (SEQ, D), jnp.float32)
    return jnp.clip(base, -6.0, 6.0).astype(jnp.bfloat16)


def draw_links(key, part):
    devices = NBLK // BLK_DEV
    width = (2 * REACH + 1) * BLK_DEV
    block = jnp.arange(NBLK, dtype=jnp.int32)[:, None]
    device = block // BLK_DEV
    offset = jnp.arange(width, dtype=jnp.int32)[None, :]
    candidate = (device - REACH) * BLK_DEV + offset
    first, second = jax.random.split(jax.random.fold_in(key, 11))
    noise = jax.random.randint(first, (NBLK, width), 0, 1 << 20)
    score = noise * 1024 + offset
    valid = (candidate >= 0) & (candidate < NBLK) & (candidate != block)
    target_device = jnp.where(device + REACH < devices, device + REACH, device - REACH)
    target = target_device * BLK_DEV + jax.random.randint(second, (NBLK, 1), 0, BLK_DEV)
    forced = (block % BLK_DEV == 0) & (candidate == target)
    score = jnp.where(valid, score, -1)
    score = jnp.where(forced, (1 << 30) + 5, score)
    chosen_score, chosen_index = lax.top_k(score, LINKS - 1)
    picked = jnp.take_along_axis(candidate, chosen_index, axis=1)
    return jnp.concatenate([block, picked], axis=1).astype(jnp.int32)


def draw_counts(key, part):
    drawn = jax.random.randint(jax.random.fold_in(key, 23), (NBLK,), 1, LINKS + 1)
    leading = jnp.arange(NBLK, dtype=jnp.int32) % BLK_DEV == 0
    drawn = jnp.where(leading, jnp.maximum(drawn, 2), drawn)
    return drawn.at[0].set(LINKS).astype(jnp.int32)


def steps_of(rng, dims, pieces, least, largest):
    def one(dim, parts):
        steps = jax.random.uniform(jax.random.fold_in(jax.random.fold_in(rng, 6), dim), (parts,), jnp.float32, least / len(pieces), largest / len(pieces))
        return jnp.repeat(jnp.exp(steps), dims[dim] // parts).reshape((-1,) + (1,) * (len(dims) - dim - 1))

    level = one(*pieces[0])
    for cut in pieces[1:]:
        level = level * one(*cut)
    return level


def length_profile(count, total, reach, lean):
    weights = [(1 << 20) // math.isqrt(standing ** lean) + 1 for standing in range(2, count + 1)]
    rest, holding = total - reach - (count - 1), [1] * (count - 1)
    while rest > 0:
        movable = [i for i in range(count - 1) if holding[i] < reach]
        whole, remaining = sum([weights[i] for i in movable]), rest
        for i in movable:
            extra = min(reach - holding[i], max(1, remaining * weights[i] // whole), rest)
            holding[i] = holding[i] + extra
            rest = rest - extra
    return np.array([reach] + holding)


def ragged_sizes(key, count, total, reach, lean):
    if count == 2:
        one = jax.random.randint(key, (), max(1, total - reach), min(reach, total - 1) + 1)
        return jnp.stack([one, total - one])
    tallies = jnp.asarray(length_profile(count, total, reach, lean), jnp.int32)
    twos = (count - 1) // 2
    donor, receiver = tallies[1:1 + 2 * twos:2], tallies[2:2 + 2 * twos:2]
    slack = jnp.minimum(donor - 1, reach - receiver)
    passed = jax.random.randint(jax.random.fold_in(key, 1), (twos,), 0, 1 << 20) % (slack + 1)
    tallies = tallies.at[1:1 + 2 * twos:2].set(donor - passed).at[2:2 + 2 * twos:2].set(receiver + passed)
    return tallies[jax.random.permutation(jax.random.fold_in(key, 2), count)]


def bell_draw(rng, extent, scale, bound, cuts=(), kind=jnp.bfloat16):
    values = scale * jax.random.normal(rng, extent, jnp.float32)
    if cuts:
        values = values * steps_of(rng, extent, cuts, -0.22, 0.18)
    return jnp.clip(values, -bound, bound).astype(kind)


def setup_inputs(seed: int = 0) -> dict:
    streams_of = jax.random.split(jax.random.key(seed), 9)
    return {
        "tokens": draw_tokens(jax.random.fold_in(streams_of[8], 71), 0),
        "query_weight": bell_draw(streams_of[1], (D, HEADS * HEAD_DIM), D ** -0.5, 0.09375, ((1, 8),)),
        "key_weight": bell_draw(streams_of[2], (D, KV_HEADS * HEAD_DIM), D ** -0.5, 0.09375, ((1, 8),)),
        "value_weight": bell_draw(streams_of[3], (D, KV_HEADS * HEAD_DIM), D ** -0.5, 0.09375, ((1, 8),)),
        "out_weight": bell_draw(streams_of[4], (HEADS * HEAD_DIM, D), (HEADS * HEAD_DIM) ** -0.5, 0.09375, ((0, 8),)),
        "links": draw_links(jax.random.fold_in(streams_of[8], 71), 0),
        "counts": draw_counts(jax.random.fold_in(streams_of[8], 71), 0),
        "doc_ids": jnp.searchsorted(jnp.cumsum(ragged_sizes(streams_of[7], DOCS, NBLK, 8, 0)), jnp.arange(NBLK), side="right").astype(jnp.int32),
    }


def reference(tokens, query_weight, key_weight, value_weight, out_weight, links, counts, doc_ids):
    query = jnp.dot(tokens, query_weight, preferred_element_type=jnp.float32).astype(jnp.bfloat16)
    keys = jnp.dot(tokens, key_weight, preferred_element_type=jnp.float32).astype(jnp.bfloat16)
    values = jnp.dot(tokens, value_weight, preferred_element_type=jnp.float32).astype(jnp.bfloat16)
    group = HEADS // KV_HEADS
    query_blocks = query.reshape(NBLK, BLOCK, KV_HEADS, group, HEAD_DIM)
    key_blocks = keys.reshape(NBLK, BLOCK, KV_HEADS, HEAD_DIM)
    value_blocks = values.reshape(NBLK, BLOCK, KV_HEADS, HEAD_DIM)
    causal = jnp.arange(BLOCK)[None, :] <= jnp.arange(BLOCK)[:, None]

    def one_block(index):
        listed = links[index]
        chosen_keys = jnp.take(key_blocks, listed, axis=0, mode="clip").astype(jnp.float32)
        chosen_values = jnp.take(value_blocks, listed, axis=0, mode="clip").astype(jnp.float32)
        live = jnp.arange(LINKS) < counts[index]
        other_doc = jnp.take(doc_ids, listed, mode="clip") != doc_ids[index]
        earlier = (listed < index) | other_doc
        same = listed == index
        allowed = live[None, :, None] & (earlier[None, :, None] | (same[None, :, None] & causal[:, None, :]))
        scores = jnp.einsum("qhgd,skhd->hgqsk", query_blocks[index].astype(jnp.float32), chosen_keys) * (HEAD_DIM ** -0.5)
        scores = jnp.where(allowed, scores, -1e30)
        top = jnp.max(scores, axis=(3, 4), keepdims=True)
        powers = jnp.where(allowed, jnp.exp(scores - top), 0.0)
        total = jnp.sum(powers, axis=(3, 4), keepdims=True)
        weights = (powers / total).astype(jnp.bfloat16).astype(jnp.float32)
        result = jnp.einsum("hgqsk,skhd->qhgd", weights, chosen_values)
        return result.astype(jnp.bfloat16)

    attended = lax.map(one_block, jnp.arange(NBLK, dtype=jnp.int32)).reshape(SEQ, HEADS * HEAD_DIM)
    width = HEADS * HEAD_DIM // N_TP
    mixed = jnp.zeros((SEQ, D), jnp.float32)
    for part_index in range(N_TP):
        term = jnp.dot(attended[:, part_index * width:(part_index + 1) * width], out_weight[part_index * width:(part_index + 1) * width], preferred_element_type=jnp.float32)
        mixed = mixed + term.astype(jnp.bfloat16).astype(jnp.float32)
    return mixed.astype(jnp.bfloat16)
```

```python
import jax
import jax.numpy as jnp
from jax import lax
from jax.experimental import pallas as pl
from jax.experimental.pallas import tpu as pltpu
from jax.sharding import PartitionSpec as P

HEAD_DIM = 128
BLOCK = 128
LINKS = 16
REACH = 4
GROUP = 4
NEG = -1e30
LOG2E = 1.4426950408889634


def along_tp(step):
    return [(t, (t + step) % 8) for t in range(8)]


SWAP = [(t, t ^ 1) for t in range(8)]


def swap(x):
    return lax.ppermute(x, "tp", SWAP)


def shift(x, chips):
    return lax.ppermute(x, "tp", along_tp(2 * chips))


def ring(x, step):
    n = lax.axis_size("ctx")
    return lax.ppermute(x, "ctx", [(i, i + step) for i in range(n) if 0 <= i + step < n])


def smem():
    return pl.BlockSpec(memory_space=pltpu.SMEM)


def vmem():
    return pl.BlockSpec(memory_space=pltpu.VMEM)


def hbm():
    return pl.BlockSpec(memory_space=pl.ANY)


def kv_kernel(order, *refs):
    xs, wk, wv, out = refs[:8], refs[8], refs[9], refs[10]
    blocks = out.shape[1]
    for w, which in ((wk, 0), (wv, 1)):
        acc = None
        for n, x in enumerate(xs):
            rows = pl.multiple_of(order[n] * x.shape[1], x.shape[1])
            part = jnp.dot(x[...], w[pl.ds(rows, x.shape[1]), :], preferred_element_type=jnp.float32)
            acc = part if acc is None else acc + part
        out[which] = acc.astype(jnp.bfloat16).reshape(blocks, BLOCK, HEAD_DIM)


def project_kv(order, xs, wk, wv):
    rows = xs[0].shape[0]
    return pl.pallas_call(
        kv_kernel,
        out_shape=jax.ShapeDtypeStruct((2, rows // BLOCK, BLOCK, HEAD_DIM), jnp.bfloat16),
        in_specs=[smem()] + [vmem()] * 10,
        out_specs=vmem(),
        cost_estimate=pl.CostEstimate(flops=rows * 4096 * 512, transcendentals=0, bytes_accessed=6 << 20),
        name="project_kv",
    )(order, *xs, wk, wv)


def q_kernel(order, *refs):
    xs, wq, out = refs[:8], refs[8], refs[9]
    acc = None
    for n, x in enumerate(xs):
        rows = pl.multiple_of(order[n] * x.shape[1], x.shape[1])
        part = jnp.dot(x[...], wq[pl.ds(rows, x.shape[1]), :], preferred_element_type=jnp.float32)
        acc = part if acc is None else acc + part
    out[...] = acc.astype(jnp.bfloat16)


def project_q(order, xs, wq):
    rows = xs[0].shape[0]
    return pl.pallas_call(
        q_kernel,
        out_shape=jax.ShapeDtypeStruct((rows, wq.shape[1]), jnp.bfloat16),
        in_specs=[smem()] + [vmem()] * 9,
        out_specs=vmem(),
        cost_estimate=pl.CostEstimate(flops=rows * 4096 * 1024, transcendentals=0, bytes_accessed=8 << 20),
        name="project_q",
    )(order, *xs, wq)


def attend_kernel(place, links, counts, docs, q, *refs):
    pieces, out = refs[:9], refs[9]
    kv, listed, many, qs, ss, mx, ls, acc, sems = refs[10:]
    for n, piece in enumerate(pieces):
        pltpu.make_async_copy(piece, kv.at[n], sems.at[n]).start()
    first = place[0] * 4
    for b in range(4):
        i = first + b
        mine = docs[i]
        n = jnp.int32(0)
        listed[b, 0] = 0
        for s in range(1, LINKS):
            j = links[b, s]
            ok = (s < counts[b]) & ((j < i) | (docs[j] != mine))
            listed[b, n] = j - first + 4 * REACH
            n = n + ok.astype(jnp.int32)
        many[b] = n
    for n, piece in enumerate(pieces):
        pltpu.make_async_copy(piece, kv.at[n], sems.at[n]).wait()
    c = LOG2E * HEAD_DIM ** (-0.5)
    nt = (((1,), (1,)), ((), ()))
    for b in range(4):
        n = many[b]
        pairs = (n + 1) // 2
        for g in range(GROUP):
            qs[pl.ds(g * BLOCK, BLOCK), :] = q[pl.ds(b * BLOCK, BLOCK), pl.ds(g * HEAD_DIM, HEAD_DIM)]
        s0 = lax.dot_general(qs[...], kv[REACH, 0, b], nt, preferred_element_type=jnp.float32)
        row = lax.broadcasted_iota(jnp.int32, s0.shape, 0) % BLOCK
        col = lax.broadcasted_iota(jnp.int32, s0.shape, 1)
        s0 = jnp.where(col <= row, s0, NEG)
        ss[LINKS // 2, :, pl.ds(0, BLOCK)] = s0
        mx[...] = s0

        def blocks(p, which):
            a = listed[b, 2 * p]
            d = listed[b, 2 * p + 1]
            return jnp.concatenate(
                [kv[a // 4, which, a % 4], kv[d // 4, which, d % 4]], axis=0
            )

        def score(p, carry):
            s = lax.dot_general(qs[...], blocks(p, 0), nt, preferred_element_type=jnp.float32)
            s1 = s[:, :BLOCK]
            s2 = jnp.where(2 * p + 1 < n, s[:, BLOCK:], NEG)
            ss[p, :, pl.ds(0, BLOCK)] = s1
            ss[p, :, pl.ds(BLOCK, BLOCK)] = s2
            mx[...] = jnp.maximum(mx[...], jnp.maximum(s1, s2))
            return carry

        listed[b, n] = 4 * REACH
        lax.fori_loop(0, pairs, score, 0)
        top = jnp.max(mx[...], axis=1, keepdims=True)
        mx[...] = jnp.broadcast_to(top, mx.shape)
        p0 = jnp.exp2((ss[LINKS // 2, :, pl.ds(0, BLOCK)] - mx[...]) * c)
        ls[...] = p0
        acc[...] = jnp.dot(p0.astype(jnp.bfloat16), kv[REACH, 1, b], preferred_element_type=jnp.float32)

        def gather(p, carry):
            m = mx[...]
            p1 = jnp.exp2((ss[p, :, pl.ds(0, BLOCK)] - m) * c)
            p2 = jnp.exp2((ss[p, :, pl.ds(BLOCK, BLOCK)] - m) * c)
            ls[...] = ls[...] + (p1 + p2)
            w = jnp.concatenate([p1.astype(jnp.bfloat16), p2.astype(jnp.bfloat16)], axis=1)
            acc[...] = acc[...] + jnp.dot(w, blocks(p, 1), preferred_element_type=jnp.float32)
            return carry

        lax.fori_loop(0, pairs, gather, 0)
        total = jnp.sum(ls[...], axis=1, keepdims=True)
        res = (acc[...] / total).astype(jnp.bfloat16)
        for g in range(GROUP):
            out[pl.ds(b * BLOCK, BLOCK), pl.ds(g * HEAD_DIM, HEAD_DIM)] = res[g * BLOCK : (g + 1) * BLOCK]


def attend(place, links, counts, docs, q, pieces):
    rows = GROUP * BLOCK
    return pl.pallas_call(
        attend_kernel,
        out_shape=jax.ShapeDtypeStruct(q.shape, jnp.bfloat16),
        in_specs=[smem()] * 4 + [vmem()] + [hbm()] * 9,
        out_specs=vmem(),
        scratch_shapes=[
            pltpu.VMEM((9, 2, 4, BLOCK, HEAD_DIM), jnp.bfloat16),
            pltpu.SMEM((4, LINKS + 2), jnp.int32),
            pltpu.SMEM((4,), jnp.int32),
            pltpu.VMEM((rows, HEAD_DIM), jnp.bfloat16),
            pltpu.VMEM((LINKS // 2 + 1, rows, 2 * BLOCK), jnp.float32),
            pltpu.VMEM((rows, BLOCK), jnp.float32),
            pltpu.VMEM((rows, BLOCK), jnp.float32),
            pltpu.VMEM((rows, HEAD_DIM), jnp.float32),
            pltpu.SemaphoreType.DMA((9,)),
        ],
        cost_estimate=pl.CostEstimate(flops=1 << 31, transcendentals=1 << 22, bytes_accessed=4 << 20),
        name="attend",
    )(place, links, counts, docs, q, *pieces)


def project_out_kernel(place, att, wo, keep, give):
    core = place[1]
    half = BLOCK // 2
    for b in range(4):
        chip = place[2 + b]
        start = pl.multiple_of(chip * BLOCK, BLOCK)
        lower = att[pl.ds(pl.multiple_of(start + core * half, half), half), :]
        upper = att[pl.ds(pl.multiple_of(start + (1 - core) * half, half), half), :]
        full = jnp.concatenate([lower, upper], axis=0)
        term = jnp.dot(full, wo[...], preferred_element_type=jnp.float32).astype(jnp.bfloat16)
        keep[b] = term[:half]
        give[b] = term[half:]


def project_out(place, att, wo):
    half = BLOCK // 2
    shape = jax.ShapeDtypeStruct((4, half, wo.shape[1]), jnp.bfloat16)
    return pl.pallas_call(
        project_out_kernel,
        out_shape=(shape, shape),
        in_specs=[smem(), vmem(), vmem()],
        out_specs=(vmem(), vmem()),
        cost_estimate=pl.CostEstimate(flops=1 << 31, transcendentals=0, bytes_accessed=9 << 20),
        name="project_out",
    )(place, att, wo)


def local(tokens, query_weight, key_weight, value_weight, out_weight, links, counts, doc_ids):
    t = lax.axis_index("tp").astype(jnp.int32)
    ctx = lax.axis_index("ctx").astype(jnp.int32)
    y, core = t // 2, t % 2
    xs = [tokens, shift(tokens, 2), shift(tokens, 1), shift(tokens, -1)]
    xs = xs + [swap(x) for x in xs]
    sources = [t, (t + 4) % 8, (t + 6) % 8, (t + 2) % 8]
    order = jnp.stack(sources + [s ^ 1 for s in sources])
    place = jnp.stack([ctx, core, (y + 2) % 4, (y + 1) % 4, (y + 3) % 4, y])
    kv = project_kv(order, xs, key_weight, value_weight)
    query = project_q(order, xs, query_weight)
    below = above = kv
    pieces = [kv]
    for _ in range(REACH):
        below, above = ring(below, 1), ring(above, -1)
        pieces = [below] + pieces + [above]
    att = attend(place, links, counts, doc_ids, query, pieces)
    keep, give = project_out(place, att, out_weight)
    got = swap(give)
    pair = keep.astype(jnp.float32) + got.astype(jnp.float32)
    far, up, down = (pair[n].astype(jnp.bfloat16) for n in range(3))
    far, up, down = shift(far, 2), shift(up, 1), shift(down, -1)
    total = pair[3] + far.astype(jnp.float32) + up.astype(jnp.float32) + down.astype(jnp.float32)
    return total.astype(jnp.bfloat16)


def solution(mesh):
    placed = (
        P("ctx", "tp"),
        P(None, "tp"),
        P(None, "tp"),
        P(None, "tp"),
        P("tp", None),
        P("ctx", None),
        P("ctx"),
        P(),
    )
    return jax.shard_map(
        local, mesh=mesh, in_specs=placed, out_specs=P(("ctx", "tp"), None), check_vma=False
    )
```

```python
import jax
import jax.numpy as jnp
from jax import lax
from jax.experimental import pallas as pl
from jax.experimental.pallas import tpu as pltpu
from jax.sharding import PartitionSpec as P

HEAD_DIM = 128
BLOCK = 128
LINKS = 16
REACH = 4
GROUP = 4
HALF = BLOCK // 2
ROWS = GROUP * BLOCK
NEG = -1e30
RATE = 1.4426950408889634 * HEAD_DIM ** (-0.5)


SWAP = [(t, t ^ 1) for t in range(8)]


def swap(x):
    return lax.ppermute(x, "tp", SWAP)


def shift(x, chips):
    return lax.ppermute(x, "tp", [(t, (t + 2 * chips) % 8) for t in range(8)])


def ring(x, step):
    n = lax.axis_size("ctx")
    return lax.ppermute(x, "ctx", [(i, i + step) for i in range(n) if 0 <= i + step < n])


def smem():
    return pl.BlockSpec(memory_space=pltpu.SMEM)


def vmem():
    return pl.BlockSpec(memory_space=pltpu.VMEM)


def limit(mib):
    return pltpu.CompilerParams(vmem_limit_bytes=mib << 20)


def chip_and_core():
    t = lax.axis_index("tp")
    return t // 2, t % 2


def destination(which):
    chip, core = chip_and_core()
    return (chip + (2, 1, 3, 0)[which]) % 4, core


def project_kernel(*refs, counts, weights, added, finish, chips):
    refs = list(refs)
    xs = []
    for c in counts:
        xs.append([refs.pop(0) for _ in range(c)])
    ws = [refs.pop(0) for _ in range(weights)]
    before = [refs.pop(0) for _ in range(weights)] if added else [None] * weights
    chip, core = chip_and_core()
    accs = [None if ref is None else ref[...] for ref in before]
    for n, parts in enumerate(xs):
        x = parts[0][...] if len(parts) == 1 else jnp.concatenate([p[...] for p in parts], axis=0)
        width = x.shape[1]
        source = 2 * ((chip + chips[n // 2]) % 4) + (core if n % 2 == 0 else 1 - core)
        first = pl.multiple_of(source * width, width)
        for k, w in enumerate(ws):
            part = jnp.dot(x, w[pl.ds(first, width), :], preferred_element_type=jnp.float32)
            accs[k] = part if accs[k] is None else accs[k] + part
    finish(refs, accs)


def project(chips, chunks, ws, before, out_shape, finish):
    flat = [part for chunk in chunks for part in chunk]
    counts = [len(chunk) for chunk in chunks]
    rows = sum(part.shape[0] for part in chunks[0])
    width = chunks[0][0].shape[1]
    cols = sum(w.shape[1] for w in ws)
    n = len(chunks)
    body = lambda *refs: project_kernel(
        *refs, counts=counts, weights=len(ws), added=bool(before), finish=finish, chips=chips
    )
    return pl.pallas_call(
        body,
        out_shape=out_shape,
        in_specs=[vmem()] * (len(flat) + len(ws) + len(before)),
        out_specs=jax.tree.map(lambda _: vmem(), out_shape),
        cost_estimate=pl.CostEstimate(
            flops=2 * rows * width * n * cols,
            transcendentals=0,
            bytes_accessed=2 * n * width * (rows + cols),
        ),
        compiler_params=limit(20),
    )(*flat, *ws, *before)


def split_kernel(up, down, first, second):
    rows = first.shape[0]
    first[...] = up[pl.ds(0, rows), :]
    second[...] = down[pl.ds(rows, rows), :]


def split(up, down):
    shape = jax.ShapeDtypeStruct((up.shape[0] // 2, up.shape[1]), up.dtype)
    return pl.pallas_call(
        split_kernel,
        out_shape=(shape, shape),
        in_specs=[vmem()] * 2,
        out_specs=(vmem(), vmem()),
        compiler_params=limit(2),
        name="split",
    )(up, down)


def add_kernel(*refs):
    total = refs[0][...].astype(jnp.float32)
    for ref in refs[1:-1]:
        total = total + ref[...].astype(jnp.float32)
    refs[-1][...] = total.astype(jnp.bfloat16)


def add(*parts):
    return pl.pallas_call(
        add_kernel,
        out_shape=jax.ShapeDtypeStruct(parts[0].shape, parts[0].dtype),
        in_specs=[vmem()] * len(parts),
        out_specs=vmem(),
        compiler_params=limit(6),
        name="add",
    )(*parts)


def keep_sums(out, accs):
    for ref, acc in zip(out, accs):
        ref[...] = acc


def store_kv(out, accs):
    kv = out[0]
    for b in range(kv.shape[1]):
        rows = slice(b * BLOCK, (b + 1) * BLOCK)
        kv[0, b] = accs[0][rows].T.astype(jnp.bfloat16)
        kv[1, b] = accs[1][rows].astype(jnp.bfloat16)


def store_q(out, accs):
    q = accs[0].astype(jnp.bfloat16)
    for b in range(q.shape[0] // BLOCK):
        for g in range(GROUP):
            out[0][b, pl.ds(g * BLOCK, BLOCK), :] = q[
                b * BLOCK : (b + 1) * BLOCK, g * HEAD_DIM : (g + 1) * HEAD_DIM
            ]


def absorb(table, line, q, below, above, m, l, acc):
    n = table[line, 0]

    def pick(kind, entry):
        return jnp.where(entry >= 4, above[kind, entry % 4], below[kind, entry % 4])

    def pair(p, carry):
        a = table[line, 1 + 2 * p]
        d = table[line, 2 + 2 * p]
        keys = jnp.concatenate([pick(0, a), pick(0, d)], axis=1)
        s = jnp.dot(q[...], keys, preferred_element_type=jnp.float32)
        s1 = s[:, :BLOCK]
        s2 = jnp.where(2 * p + 1 < n, s[:, BLOCK:], NEG)
        old = m[...]
        new = jnp.maximum(old, jnp.max(jnp.maximum(s1, s2), axis=1, keepdims=True))
        m[...] = new
        fade = jnp.exp2((old - new) * RATE)
        p1 = jnp.exp2((s1 - new) * RATE)
        p2 = jnp.exp2((s2 - new) * RATE)
        l[...] = l[...] * fade + (p1 + p2)
        w = jnp.concatenate([p1.astype(jnp.bfloat16), p2.astype(jnp.bfloat16)], axis=1)
        values = jnp.concatenate([pick(1, a), pick(1, d)], axis=0)
        acc[...] = acc[...] * fade + jnp.dot(w, values, preferred_element_type=jnp.float32)
        return carry

    lax.fori_loop(0, (n + 1) // 2, pair, 0)


def table_kernel(links, counts, docs, table):
    ctx = lax.axis_index("ctx")
    for line in range(5 * 4):
        table[line, 0] = 0
    for b in range(4):
        i = ctx * 4 + b
        mine = docs[i]
        live = counts[b]
        for s in range(1, LINKS):
            j = links[b, s]
            away = j // 4 - ctx
            line = jnp.abs(away) * 4 + b
            at = table[line, 0]
            ok = (s < live) & ((j < i) | (docs[j] != mine))
            table[line, 1 + at] = jnp.where(away > 0, 4, 0) + j % 4
            table[line, 0] = at + ok.astype(jnp.int32)
    for line in range(5 * 4):
        table[line, 1 + table[line, 0]] = 0


def list_slots(links, counts, docs):
    return pl.pallas_call(
        table_kernel,
        out_shape=jax.ShapeDtypeStruct((5 * 4, LINKS + 2), jnp.int32),
        in_specs=[smem()] * 3,
        out_specs=smem(),
        compiler_params=limit(1),
        name="list_slots",
    )(links, counts, docs)


def begin(q, own, b, m, l, acc):
    s = jnp.dot(q[...], own[0, b], preferred_element_type=jnp.float32)
    row = lax.broadcasted_iota(jnp.int32, s.shape, 0) % BLOCK
    col = lax.broadcasted_iota(jnp.int32, s.shape, 1)
    s = jnp.where(col <= row, s, NEG)
    top = jnp.broadcast_to(jnp.max(s, axis=1, keepdims=True), s.shape)
    w = jnp.exp2((s - top) * RATE)
    m[...] = top
    l[...] = w
    acc[...] = jnp.dot(w.astype(jnp.bfloat16), own[1, b], preferred_element_type=jnp.float32)


def close(core, l, acc, wo, keep, give, wide):
    total = jnp.sum(l[...], axis=1, keepdims=True)
    res = (acc[...] / total).astype(jnp.bfloat16)
    for g in range(GROUP):
        wide[:, pl.ds(g * HEAD_DIM, HEAD_DIM)] = res[g * BLOCK : (g + 1) * BLOCK]
    mine = wide[pl.ds(pl.multiple_of(core * HALF, HALF), HALF), :]
    other = wide[pl.ds(pl.multiple_of((1 - core) * HALF, HALF), HALF), :]
    both = jnp.concatenate([mine, other], axis=0)
    term = jnp.dot(both, wo[...], preferred_element_type=jnp.float32).astype(jnp.bfloat16)
    keep[...] = term[:HALF]
    give[...] = term[HALF:]


def attend_kernel(table, q, *refs, which, steps, starts, ends):
    refs = list(refs)
    b, core = destination(which)
    q = q.at[b]
    own = refs.pop(0) if 0 in steps else None
    pieces = {k: (refs.pop(0), refs.pop(0)) for k in steps if k}
    state0 = [] if starts else [refs.pop(0) for _ in range(3)]
    wo = refs.pop(0) if ends else None
    if ends:
        keep, give, m, l, acc, wide = refs
    else:
        m, l, acc = refs
    if starts:
        begin(q, own, b, m, l, acc)
    else:
        for now, past in zip((m, l, acc), state0):
            now[...] = past[...]
    for k in steps:
        below, above = pieces[k] if k else (own, own)
        absorb(table, 4 * k + b, q, below, above, m, l, acc)
    if ends:
        close(core, l, acc, wo, keep, give, wide)


def attend(table, q, which, pieces, state, wo):
    steps = sorted(pieces)
    flat = [piece for k in steps for piece in pieces[k]]
    starts, ends = state is None, wo is not None
    one = jax.ShapeDtypeStruct((ROWS, HEAD_DIM), jnp.float32)
    scratch = [pltpu.VMEM((ROWS, HEAD_DIM), jnp.float32)] * 3
    if ends:
        out_shape = (jax.ShapeDtypeStruct((HALF, wo.shape[1]), jnp.bfloat16),) * 2
        scratch = scratch + [pltpu.VMEM((BLOCK, GROUP * HEAD_DIM), jnp.bfloat16)]
    else:
        out_shape, scratch = (one,) * 3, []
    args = flat + ([] if starts else list(state)) + ([wo] if ends else [])
    return pl.pallas_call(
        lambda *refs: attend_kernel(
            *refs, which=which, steps=steps, starts=starts, ends=ends
        ),
        out_shape=out_shape,
        in_specs=[smem()] + [vmem()] * (1 + len(args)),
        out_specs=(vmem(),) * len(out_shape),
        scratch_shapes=scratch,
        cost_estimate=pl.CostEstimate(
            flops=1 << 29, transcendentals=1 << 20, bytes_accessed=4 << 20
        ),
        compiler_params=limit(16),
    )(table, q, *args)


def layer(tokens, query_weight, key_weight, value_weight, out_weight, links, counts, doc_ids):
    rows = tokens.shape[0]
    table = list_slots(links, counts, doc_ids)

    up, down = shift(tokens, 1), shift(tokens, -1)
    twin = swap(tokens)
    halves = split(up, down)
    far = [shift(halves[0], 1), shift(halves[1], -1)]
    first = [[tokens], [twin], [up], [swap(up)], [down], [swap(down)]]
    second = [far, [swap(far[0]), swap(far[1])]]

    sums = lambda *cols: tuple(jax.ShapeDtypeStruct((rows, n), jnp.float32) for n in cols)
    kv_weights = [key_weight, value_weight]
    *kv_sums, q_sums = project(
        (0, 3, 1), first, kv_weights + [query_weight], [], sums(128, 128, 512), keep_sums
    )
    kv_shape = (jax.ShapeDtypeStruct((2, rows // BLOCK, BLOCK, HEAD_DIM), jnp.bfloat16),)
    kv = project((2,), second, kv_weights, kv_sums, kv_shape, store_kv)[0]
    q_shape = (jax.ShapeDtypeStruct((rows // BLOCK, ROWS, HEAD_DIM), jnp.bfloat16),)
    q = project((2,), second, [query_weight], [q_sums], q_shape, store_q)[0]

    pieces = {0: (kv,)}
    below = above = kv
    for k in range(1, REACH + 1):
        below, above = ring(below, 1), ring(above, -1)
        pieces[k] = below, above
    early = {k: pieces[k] for k in range(REACH)}
    state = attend(table, q, 0, early, None, None)
    whole = lambda which: attend(table, q, which, pieces, None, out_weight)
    merge = lambda pair: add(pair[0], swap(pair[1]))

    pair = attend(table, q, 0, {REACH: pieces[REACH]}, state, out_weight)
    across = shift(merge(pair), 2)
    from_below = shift(merge(whole(1)), 1)
    from_above = shift(merge(whole(2)), -1)
    keep, give = whole(3)
    return add(keep, swap(give), across, from_below, from_above)


def solution(mesh):
    placed = (
        P("ctx", "tp"),
        P(None, "tp"),
        P(None, "tp"),
        P(None, "tp"),
        P("tp", None),
        P("ctx", None),
        P("ctx"),
        P(),
    )
    return jax.shard_map(
        layer, mesh=mesh, in_specs=placed, out_specs=P(("ctx", "tp"), None), check_vma=False
    )
```

```python
import jax
import jax.numpy as jnp
from jax import lax
from jax.experimental import pallas as pl
from jax.experimental.pallas import tpu as pltpu
from jax.sharding import PartitionSpec as P

HEAD_DIM = 128
BLOCK = 128
LINKS = 16
REACH = 4
GROUP = 4
HALF = BLOCK // 2
ROWS = GROUP * BLOCK
NEG = -1e30
RATE = 1.4426950408889634 * HEAD_DIM ** (-0.5)


SWAP = [(t, t ^ 1) for t in range(8)]


def swap(x):
    return lax.ppermute(x, "tp", SWAP)


def shift(x, chips):
    return lax.ppermute(x, "tp", [(t, (t + 2 * chips) % 8) for t in range(8)])


def ring(x, step):
    n = lax.axis_size("ctx")
    return lax.ppermute(x, "ctx", [(i, i + step) for i in range(n) if 0 <= i + step < n])


def smem():
    return pl.BlockSpec(memory_space=pltpu.SMEM)


def vmem():
    return pl.BlockSpec(memory_space=pltpu.VMEM)


def limit(mib):
    return pltpu.CompilerParams(vmem_limit_bytes=mib << 20)


def chip_and_core():
    t = lax.axis_index("tp")
    return t // 2, t % 2


def destination(which):
    chip, core = chip_and_core()
    return (chip + (2, 1, 3, 0)[which]) % 4, core


def project_kernel(*refs, counts, weights, added, finish, chips):
    refs = list(refs)
    xs = []
    for c in counts:
        xs.append([refs.pop(0) for _ in range(c)])
    ws = [refs.pop(0) for _ in range(weights)]
    before = [refs.pop(0) for _ in range(weights)] if added else [None] * weights
    chip, core = chip_and_core()
    accs = [None if ref is None else ref[...] for ref in before]
    for n, parts in enumerate(xs):
        x = parts[0][...] if len(parts) == 1 else jnp.concatenate([p[...] for p in parts], axis=0)
        width = x.shape[1]
        source = 2 * ((chip + chips[n // 2]) % 4) + (core if n % 2 == 0 else 1 - core)
        first = pl.multiple_of(source * width, width)
        for k, w in enumerate(ws):
            part = jnp.dot(x, w[pl.ds(first, width), :], preferred_element_type=jnp.float32)
            accs[k] = part if accs[k] is None else accs[k] + part
    finish(refs, accs)


def project(chips, chunks, ws, before, out_shape, finish):
    flat = [part for chunk in chunks for part in chunk]
    counts = [len(chunk) for chunk in chunks]
    rows = sum(part.shape[0] for part in chunks[0])
    width = chunks[0][0].shape[1]
    cols = sum(w.shape[1] for w in ws)
    n = len(chunks)
    body = lambda *refs: project_kernel(
        *refs, counts=counts, weights=len(ws), added=bool(before), finish=finish, chips=chips
    )
    return pl.pallas_call(
        body,
        out_shape=out_shape,
        in_specs=[vmem()] * (len(flat) + len(ws) + len(before)),
        out_specs=jax.tree.map(lambda _: vmem(), out_shape),
        cost_estimate=pl.CostEstimate(
            flops=2 * rows * width * n * cols,
            transcendentals=0,
            bytes_accessed=2 * n * width * (rows + cols),
        ),
        compiler_params=limit(20),
    )(*flat, *ws, *before)


def half_of(x, second):
    rows = x.shape[0] // 2

    def body(x, out):
        out[...] = x[pl.ds(rows if second else 0, rows), :]

    return pl.pallas_call(
        body,
        out_shape=jax.ShapeDtypeStruct((rows, x.shape[1]), x.dtype),
        in_specs=[vmem()],
        out_specs=vmem(),
        compiler_params=limit(2),
    )(x)


def load_kernel(*refs):
    n = len(refs) // 2
    sems = refs[-1]
    copies = [pltpu.make_async_copy(refs[k], refs[n + k], sems.at[k]) for k in range(n)]
    for copy in copies:
        copy.start()
    for copy in copies:
        copy.wait()


def load(*arrays):
    return pl.pallas_call(
        load_kernel,
        out_shape=tuple(jax.ShapeDtypeStruct(x.shape, x.dtype) for x in arrays),
        in_specs=[pl.BlockSpec(memory_space=pltpu.HBM)] * len(arrays),
        out_specs=(vmem(),) * len(arrays),
        scratch_shapes=[pltpu.SemaphoreType.DMA((len(arrays),))],
        compiler_params=limit(12),
        name="load",
    )(*arrays)


def add_kernel(*refs):
    total = refs[0][...].astype(jnp.float32)
    for ref in refs[1:-1]:
        total = total + ref[...].astype(jnp.float32)
    refs[-1][...] = total.astype(jnp.bfloat16)


def add(*parts):
    return pl.pallas_call(
        add_kernel,
        out_shape=jax.ShapeDtypeStruct(parts[0].shape, parts[0].dtype),
        in_specs=[vmem()] * len(parts),
        out_specs=vmem(),
        compiler_params=limit(6),
        name="add",
    )(*parts)


def keep_sums(out, accs):
    for ref, acc in zip(out, accs):
        ref[...] = acc


def store_kv(out, accs):
    kv = out[0]
    for b in range(kv.shape[1]):
        rows = slice(b * BLOCK, (b + 1) * BLOCK)
        kv[0, b] = accs[0][rows].T.astype(jnp.bfloat16)
        kv[1, b] = accs[1][rows].astype(jnp.bfloat16)


def store_q(out, accs):
    q = accs[0].astype(jnp.bfloat16)
    for b in range(q.shape[0] // BLOCK):
        for g in range(GROUP):
            out[0][b, pl.ds(g * BLOCK, BLOCK), :] = q[
                b * BLOCK : (b + 1) * BLOCK, g * HEAD_DIM : (g + 1) * HEAD_DIM
            ]


def absorb(table, line, q, below, above, m, l, acc):
    n = table[line, 0]

    def pick(kind, entry):
        return jnp.where(entry >= 4, above[kind, entry % 4], below[kind, entry % 4])

    def pair(p, carry):
        a = table[line, 1 + 2 * p]
        d = table[line, 2 + 2 * p]
        keys = jnp.concatenate([pick(0, a), pick(0, d)], axis=1)
        s = jnp.dot(q[...], keys, preferred_element_type=jnp.float32)
        s1 = s[:, :BLOCK]
        s2 = jnp.where(2 * p + 1 < n, s[:, BLOCK:], NEG)
        old = m[...]
        new = jnp.maximum(old, jnp.max(jnp.maximum(s1, s2), axis=1, keepdims=True))
        m[...] = new
        fade = jnp.exp2((old - new) * RATE)
        p1 = jnp.exp2((s1 - new) * RATE)
        p2 = jnp.exp2((s2 - new) * RATE)
        l[...] = l[...] * fade + (p1 + p2)
        w = jnp.concatenate([p1.astype(jnp.bfloat16), p2.astype(jnp.bfloat16)], axis=1)
        values = jnp.concatenate([pick(1, a), pick(1, d)], axis=0)
        acc[...] = acc[...] * fade + jnp.dot(w, values, preferred_element_type=jnp.float32)
        return carry

    lax.fori_loop(0, (n + 1) // 2, pair, 0)


def table_kernel(links, counts, docs, table):
    ctx = lax.axis_index("ctx")
    for line in range(5 * 4):
        table[line, 0] = 0
    for b in range(4):
        i = ctx * 4 + b
        mine = docs[i]
        live = counts[b]
        for s in range(1, LINKS):
            j = links[b, s]
            away = j // 4 - ctx
            line = jnp.abs(away) * 4 + b
            at = table[line, 0]
            ok = (s < live) & ((j < i) | (docs[j] != mine))
            table[line, 1 + at] = jnp.where(away > 0, 4, 0) + j % 4
            table[line, 0] = at + ok.astype(jnp.int32)
    for line in range(5 * 4):
        table[line, 1 + table[line, 0]] = 0


def list_slots(links, counts, docs):
    return pl.pallas_call(
        table_kernel,
        out_shape=jax.ShapeDtypeStruct((5 * 4, LINKS + 2), jnp.int32),
        in_specs=[smem()] * 3,
        out_specs=smem(),
        compiler_params=limit(1),
        name="list_slots",
    )(links, counts, docs)


def begin(q, own, b, m, l, acc):
    s = jnp.dot(q[...], own[0, b], preferred_element_type=jnp.float32)
    row = lax.broadcasted_iota(jnp.int32, s.shape, 0) % BLOCK
    col = lax.broadcasted_iota(jnp.int32, s.shape, 1)
    s = jnp.where(col <= row, s, NEG)
    top = jnp.broadcast_to(jnp.max(s, axis=1, keepdims=True), s.shape)
    w = jnp.exp2((s - top) * RATE)
    m[...] = top
    l[...] = w
    acc[...] = jnp.dot(w.astype(jnp.bfloat16), own[1, b], preferred_element_type=jnp.float32)


def close(core, l, acc, wo, keep, give, wide):
    total = jnp.sum(l[...], axis=1, keepdims=True)
    res = (acc[...] / total).astype(jnp.bfloat16)
    for g in range(GROUP):
        wide[:, pl.ds(g * HEAD_DIM, HEAD_DIM)] = res[g * BLOCK : (g + 1) * BLOCK]
    mine = wide[pl.ds(pl.multiple_of(core * HALF, HALF), HALF), :]
    other = wide[pl.ds(pl.multiple_of((1 - core) * HALF, HALF), HALF), :]
    both = jnp.concatenate([mine, other], axis=0)
    term = jnp.dot(both, wo[...], preferred_element_type=jnp.float32).astype(jnp.bfloat16)
    keep[...] = term[:HALF]
    give[...] = term[HALF:]


def attend_kernel(table, q, *refs, which, steps, starts, ends):
    refs = list(refs)
    b, core = destination(which)
    q = q.at[b]
    own = refs.pop(0) if 0 in steps else None
    pieces = {k: (refs.pop(0), refs.pop(0)) for k in steps if k}
    state0 = [] if starts else [refs.pop(0) for _ in range(3)]
    wo = refs.pop(0) if ends else None
    if ends:
        keep, give, m, l, acc, wide = refs
    else:
        m, l, acc = refs
    if starts:
        begin(q, own, b, m, l, acc)
    else:
        for now, past in zip((m, l, acc), state0):
            now[...] = past[...]
    for k in steps:
        below, above = pieces[k] if k else (own, own)
        absorb(table, 4 * k + b, q, below, above, m, l, acc)
    if ends:
        close(core, l, acc, wo, keep, give, wide)


def attend(table, q, which, pieces, state, wo):
    steps = sorted(pieces)
    flat = [piece for k in steps for piece in pieces[k]]
    starts, ends = state is None, wo is not None
    one = jax.ShapeDtypeStruct((ROWS, HEAD_DIM), jnp.float32)
    scratch = [pltpu.VMEM((ROWS, HEAD_DIM), jnp.float32)] * 3
    if ends:
        out_shape = (jax.ShapeDtypeStruct((HALF, wo.shape[1]), jnp.bfloat16),) * 2
        scratch = scratch + [pltpu.VMEM((BLOCK, GROUP * HEAD_DIM), jnp.bfloat16)]
    else:
        out_shape, scratch = (one,) * 3, []
    args = flat + ([] if starts else list(state)) + ([wo] if ends else [])
    return pl.pallas_call(
        lambda *refs: attend_kernel(
            *refs, which=which, steps=steps, starts=starts, ends=ends
        ),
        out_shape=out_shape,
        in_specs=[smem()] + [vmem()] * (1 + len(args)),
        out_specs=(vmem(),) * len(out_shape),
        scratch_shapes=scratch,
        cost_estimate=pl.CostEstimate(
            flops=1 << 29, transcendentals=1 << 20, bytes_accessed=4 << 20
        ),
        compiler_params=limit(16),
    )(table, q, *args)


def layer(tokens, query_weight, key_weight, value_weight, out_weight, links, counts, doc_ids):
    rows = tokens.shape[0]
    table = list_slots(links, counts, doc_ids)

    up, down = shift(tokens, 1), shift(tokens, -1)
    twin = swap(tokens)
    key_weight, value_weight, query_weight, mine = load(key_weight, value_weight, query_weight, tokens)
    far_down = shift(half_of(down, True), -1)
    far = [shift(half_of(up, False), 1), far_down]
    first = [[mine], [twin], [up], [swap(up)], [down], [swap(down)]]
    second = [far, [swap(far[0]), swap(far[1])]]

    sums = lambda *cols: tuple(jax.ShapeDtypeStruct((rows, n), jnp.float32) for n in cols)
    kv_weights = [key_weight, value_weight]
    *kv_sums, q_sums = project(
        (0, 3, 1), first, kv_weights + [query_weight], [], sums(128, 128, 512), keep_sums
    )
    kv_shape = (jax.ShapeDtypeStruct((2, rows // BLOCK, BLOCK, HEAD_DIM), jnp.bfloat16),)
    kv = project((2,), second, kv_weights, kv_sums, kv_shape, store_kv)[0]
    q_shape = (jax.ShapeDtypeStruct((rows // BLOCK, ROWS, HEAD_DIM), jnp.bfloat16),)
    q = project((2,), second, [query_weight], [q_sums], q_shape, store_q)[0]

    pieces = {0: (kv,)}
    below = above = kv
    for k in range(1, REACH + 1):
        below, above = ring(below, 1), ring(above, -1)
        pieces[k] = below, above
    merge = lambda pair: add(pair[0], swap(pair[1]))

    def two_parts(which, cut):
        parts = {k: pieces[k] for k in range(cut)}, {k: pieces[k] for k in range(cut, REACH + 1)}
        state = attend(table, q, which, parts[0], None, None)
        return attend(table, q, which, parts[1], state, out_weight)

    across = shift(merge(two_parts(0, 4)), 2)
    from_below = shift(merge(two_parts(1, 2)), 1)
    from_above = shift(merge(two_parts(2, 3)), -1)
    keep, give = attend(table, q, 3, pieces, None, out_weight)
    return add(keep, swap(give), across, from_below, from_above)


def solution(mesh):
    placed = (
        P("ctx", "tp"),
        P(None, "tp"),
        P(None, "tp"),
        P(None, "tp"),
        P("tp", None),
        P("ctx", None),
        P("ctx"),
        P(),
    )
    return jax.shard_map(
        layer, mesh=mesh, in_specs=placed, out_specs=P(("ctx", "tp"), None), check_vma=False
    )
```

```python
import jax
import jax.numpy as jnp
from jax import lax
from jax.experimental import pallas as pl
from jax.experimental.pallas import tpu as pltpu
from jax.sharding import PartitionSpec as P

HEAD_DIM = 128
BLOCK = 128
LINKS = 16
REACH = 4
GROUP = 4
HALF = BLOCK // 2
ROWS = GROUP * BLOCK
NEG = -1e30
RATE = 1.4426950408889634 * HEAD_DIM ** (-0.5)


SWAP = [(t, t ^ 1) for t in range(8)]


def swap(x):
    return lax.ppermute(x, "tp", SWAP)


def across_y(x, mask):
    return lax.ppermute(x, "tp", [(t, t ^ (2 * mask)) for t in range(8)])


def exchange(x, first):
    route = []
    for c in range(first, lax.axis_size("ctx") - 1, 2):
        route += [(c, c + 1), (c + 1, c)]
    return lax.ppermute(x, "ctx", route)


def smem():
    return pl.BlockSpec(memory_space=pltpu.SMEM)


def vmem():
    return pl.BlockSpec(memory_space=pltpu.VMEM)


def limit(mib):
    return pltpu.CompilerParams(vmem_limit_bytes=mib << 20)


def chip_and_core():
    t = lax.axis_index("tp")
    return t // 2, t % 2


def destination(which):
    chip, core = chip_and_core()
    return chip ^ (2, 1, 3, 0)[which], core


def project_kernel(*refs, counts, weights, added, finish, chips):
    refs = list(refs)
    xs = []
    for c in counts:
        xs.append([refs.pop(0) for _ in range(c)])
    ws = [refs.pop(0) for _ in range(weights)]
    before = [refs.pop(0) for _ in range(weights)] if added else [None] * weights
    chip, core = chip_and_core()
    accs = [None if ref is None else ref[...] for ref in before]
    for n, parts in enumerate(xs):
        x = parts[0][...] if len(parts) == 1 else jnp.concatenate([p[...] for p in parts], axis=0)
        width = x.shape[1]
        source = 2 * (chip ^ chips[n // 2]) + (core if n % 2 == 0 else 1 - core)
        first = pl.multiple_of(source * width, width)
        for k, w in enumerate(ws):
            part = jnp.dot(x, w[pl.ds(first, width), :], preferred_element_type=jnp.float32)
            accs[k] = part if accs[k] is None else accs[k] + part
    finish(refs, accs)


def project(chips, chunks, ws, before, out_shape, finish):
    flat = [part for chunk in chunks for part in chunk]
    counts = [len(chunk) for chunk in chunks]
    rows = sum(part.shape[0] for part in chunks[0])
    width = chunks[0][0].shape[1]
    cols = sum(w.shape[1] for w in ws)
    n = len(chunks)
    body = lambda *refs: project_kernel(
        *refs, counts=counts, weights=len(ws), added=bool(before), finish=finish, chips=chips
    )
    return pl.pallas_call(
        body,
        out_shape=out_shape,
        in_specs=[vmem()] * (len(flat) + len(ws) + len(before)),
        out_specs=jax.tree.map(lambda _: vmem(), out_shape),
        cost_estimate=pl.CostEstimate(
            flops=2 * rows * width * n * cols,
            transcendentals=0,
            bytes_accessed=2 * n * width * (rows + cols),
        ),
        compiler_params=limit(20),
    )(*flat, *ws, *before)


def half_of(x, second):
    rows = x.shape[0] // 2

    def body(x, out):
        out[...] = x[pl.ds(rows if second else 0, rows), :]

    return pl.pallas_call(
        body,
        out_shape=jax.ShapeDtypeStruct((rows, x.shape[1]), x.dtype),
        in_specs=[vmem()],
        out_specs=vmem(),
        compiler_params=limit(2),
    )(x)


def load_kernel(*refs):
    n = len(refs) // 2
    sems = refs[-1]
    copies = [pltpu.make_async_copy(refs[k], refs[n + k], sems.at[k]) for k in range(n)]
    for copy in copies:
        copy.start()
    for copy in copies:
        copy.wait()


def load(*arrays):
    return pl.pallas_call(
        load_kernel,
        out_shape=tuple(jax.ShapeDtypeStruct(x.shape, x.dtype) for x in arrays),
        in_specs=[pl.BlockSpec(memory_space=pltpu.HBM)] * len(arrays),
        out_specs=(vmem(),) * len(arrays),
        scratch_shapes=[pltpu.SemaphoreType.DMA((len(arrays),))],
        compiler_params=limit(12),
        name="load",
    )(*arrays)


def add_kernel(*refs):
    total = refs[0][...].astype(jnp.float32)
    for ref in refs[1:-1]:
        total = total + ref[...].astype(jnp.float32)
    refs[-1][...] = total.astype(jnp.bfloat16)


def add(*parts):
    return pl.pallas_call(
        add_kernel,
        out_shape=jax.ShapeDtypeStruct(parts[0].shape, parts[0].dtype),
        in_specs=[vmem()] * len(parts),
        out_specs=vmem(),
        compiler_params=limit(6),
        name="add",
    )(*parts)


def keep_sums(out, accs):
    for ref, acc in zip(out, accs):
        ref[...] = acc


def store_kv(out, accs):
    kv = out[0]
    for b in range(kv.shape[1]):
        rows = slice(b * BLOCK, (b + 1) * BLOCK)
        kv[0, b] = accs[0][rows].T.astype(jnp.bfloat16)
        kv[1, b] = accs[1][rows].astype(jnp.bfloat16)


def store_q(out, accs):
    q = accs[0].astype(jnp.bfloat16)
    for b in range(q.shape[0] // BLOCK):
        for g in range(GROUP):
            out[0][b, pl.ds(g * BLOCK, BLOCK), :] = q[
                b * BLOCK : (b + 1) * BLOCK, g * HEAD_DIM : (g + 1) * HEAD_DIM
            ]


def absorb(table, line, q, below, above, m, l, acc):
    n = table[line, 0]

    def pick(kind, entry):
        return jnp.where(entry >= 4, above[kind, entry % 4], below[kind, entry % 4])

    def pair(p, carry):
        a = table[line, 1 + 2 * p]
        d = table[line, 2 + 2 * p]
        keys = jnp.concatenate([pick(0, a), pick(0, d)], axis=1)
        s = jnp.dot(q[...], keys, preferred_element_type=jnp.float32)
        s1 = s[:, :BLOCK]
        s2 = jnp.where(2 * p + 1 < n, s[:, BLOCK:], NEG)
        old = m[...]
        new = jnp.maximum(old, jnp.max(jnp.maximum(s1, s2), axis=1, keepdims=True))
        m[...] = new
        fade = jnp.exp2((old - new) * RATE)
        p1 = jnp.exp2((s1 - new) * RATE)
        p2 = jnp.exp2((s2 - new) * RATE)
        l[...] = l[...] * fade + (p1 + p2)
        w = jnp.concatenate([p1.astype(jnp.bfloat16), p2.astype(jnp.bfloat16)], axis=1)
        values = jnp.concatenate([pick(1, a), pick(1, d)], axis=0)
        acc[...] = acc[...] * fade + jnp.dot(w, values, preferred_element_type=jnp.float32)
        return carry

    lax.fori_loop(0, (n + 1) // 2, pair, 0)


def table_kernel(links, counts, docs, table):
    ctx = lax.axis_index("ctx")
    for line in range(5 * 4):
        table[line, 0] = 0
    for b in range(4):
        i = ctx * 4 + b
        mine = docs[i]
        live = counts[b]
        for s in range(1, LINKS):
            j = links[b, s]
            away = j // 4 - ctx
            line = jnp.abs(away) * 4 + b
            at = table[line, 0]
            ok = (s < live) & ((j < i) | (docs[j] != mine))
            table[line, 1 + at] = jnp.where((away > 0) == (ctx % 2 == 1), 4, 0) + j % 4
            table[line, 0] = at + ok.astype(jnp.int32)
    for line in range(5 * 4):
        table[line, 1 + table[line, 0]] = 0


def list_slots(links, counts, docs):
    return pl.pallas_call(
        table_kernel,
        out_shape=jax.ShapeDtypeStruct((5 * 4, LINKS + 2), jnp.int32),
        in_specs=[smem()] * 3,
        out_specs=smem(),
        compiler_params=limit(1),
        name="list_slots",
    )(links, counts, docs)


def begin(q, own, b, m, l, acc):
    s = jnp.dot(q[...], own[0, b], preferred_element_type=jnp.float32)
    row = lax.broadcasted_iota(jnp.int32, s.shape, 0) % BLOCK
    col = lax.broadcasted_iota(jnp.int32, s.shape, 1)
    s = jnp.where(col <= row, s, NEG)
    top = jnp.broadcast_to(jnp.max(s, axis=1, keepdims=True), s.shape)
    w = jnp.exp2((s - top) * RATE)
    m[...] = top
    l[...] = w
    acc[...] = jnp.dot(w.astype(jnp.bfloat16), own[1, b], preferred_element_type=jnp.float32)


def close(core, l, acc, wo, keep, give, wide):
    total = jnp.sum(l[...], axis=1, keepdims=True)
    res = (acc[...] / total).astype(jnp.bfloat16)
    for g in range(GROUP):
        wide[:, pl.ds(g * HEAD_DIM, HEAD_DIM)] = res[g * BLOCK : (g + 1) * BLOCK]
    mine = wide[pl.ds(pl.multiple_of(core * HALF, HALF), HALF), :]
    other = wide[pl.ds(pl.multiple_of((1 - core) * HALF, HALF), HALF), :]
    both = jnp.concatenate([mine, other], axis=0)
    term = jnp.dot(both, wo[...], preferred_element_type=jnp.float32).astype(jnp.bfloat16)
    keep[...] = term[:HALF]
    give[...] = term[HALF:]


def attend_kernel(table, q, *refs, which, steps, starts, ends):
    refs = list(refs)
    b, core = destination(which)
    q = q.at[b]
    own = refs.pop(0) if 0 in steps else None
    pieces = {k: (refs.pop(0), refs.pop(0)) for k in steps if k}
    state0 = [] if starts else [refs.pop(0) for _ in range(3)]
    wo = refs.pop(0) if ends else None
    if ends:
        keep, give, m, l, acc, wide = refs
    else:
        m, l, acc = refs
    if starts:
        begin(q, own, b, m, l, acc)
    else:
        for now, past in zip((m, l, acc), state0):
            now[...] = past[...]
    for k in steps:
        below, above = pieces[k] if k else (own, own)
        absorb(table, 4 * k + b, q, below, above, m, l, acc)
    if ends:
        close(core, l, acc, wo, keep, give, wide)


def attend(table, q, which, pieces, state, wo):
    steps = sorted(pieces)
    flat = [piece for k in steps for piece in pieces[k]]
    starts, ends = state is None, wo is not None
    one = jax.ShapeDtypeStruct((ROWS, HEAD_DIM), jnp.float32)
    scratch = [pltpu.VMEM((ROWS, HEAD_DIM), jnp.float32)] * 3
    if ends:
        out_shape = (jax.ShapeDtypeStruct((HALF, wo.shape[1]), jnp.bfloat16),) * 2
        scratch = scratch + [pltpu.VMEM((BLOCK, GROUP * HEAD_DIM), jnp.bfloat16)]
    else:
        out_shape, scratch = (one,) * 3, []
    args = flat + ([] if starts else list(state)) + ([wo] if ends else [])
    return pl.pallas_call(
        lambda *refs: attend_kernel(
            *refs, which=which, steps=steps, starts=starts, ends=ends
        ),
        out_shape=out_shape,
        in_specs=[smem()] + [vmem()] * (1 + len(args)),
        out_specs=(vmem(),) * len(out_shape),
        scratch_shapes=scratch,
        cost_estimate=pl.CostEstimate(
            flops=1 << 29, transcendentals=1 << 20, bytes_accessed=4 << 20
        ),
        compiler_params=limit(16),
    )(table, q, *args)


def layer(tokens, query_weight, key_weight, value_weight, out_weight, links, counts, doc_ids):
    rows = tokens.shape[0]
    table = list_slots(links, counts, doc_ids)

    up, down = across_y(tokens, 1), across_y(tokens, 3)
    twin = swap(tokens)
    key_weight, value_weight, query_weight, mine = load(key_weight, value_weight, query_weight, tokens)
    far_up = across_y(half_of(down, True), 1)
    far_down = across_y(half_of(up, False), 3)
    far = [far_down, far_up]
    first = [[mine], [twin], [up], [swap(up)], [down], [swap(down)]]
    second = [far, [swap(far_down), swap(far_up)]]

    sums = lambda *cols: tuple(jax.ShapeDtypeStruct((rows, n), jnp.float32) for n in cols)
    kv_weights = [key_weight, value_weight]
    *kv_sums, q_sums = project(
        (0, 1, 3), first, kv_weights + [query_weight], [], sums(128, 128, 512), keep_sums
    )
    kv_shape = (jax.ShapeDtypeStruct((2, rows // BLOCK, BLOCK, HEAD_DIM), jnp.bfloat16),)
    kv = project((2,), second, kv_weights, kv_sums, kv_shape, store_kv)[0]
    q_shape = (jax.ShapeDtypeStruct((rows // BLOCK, ROWS, HEAD_DIM), jnp.bfloat16),)
    q = project((2,), second, [query_weight], [q_sums], q_shape, store_q)[0]

    pieces = {0: (kv,)}
    even = odd = kv
    for k in range(1, REACH + 1):
        even, odd = exchange(odd, 0), exchange(even, 1)
        pieces[k] = even, odd
    merge = lambda pair: add(pair[0], swap(pair[1]))

    def two_parts(which, cut):
        parts = {k: pieces[k] for k in range(cut)}, {k: pieces[k] for k in range(cut, REACH + 1)}
        state = attend(table, q, which, parts[0], None, None)
        return attend(table, q, which, parts[1], state, out_weight)

    across = across_y(merge(two_parts(0, 4)), 2)
    from_below = across_y(merge(two_parts(1, 2)), 1)
    from_above = across_y(merge(two_parts(2, 3)), 3)
    keep, give = attend(table, q, 3, pieces, None, out_weight)
    return add(keep, swap(give), across, from_below, from_above)


def solution(mesh):
    placed = (
        P("ctx", "tp"),
        P(None, "tp"),
        P(None, "tp"),
        P(None, "tp"),
        P("tp", None),
        P("ctx", None),
        P("ctx"),
        P(),
    )
    return jax.shard_map(
        layer, mesh=mesh, in_specs=placed, out_specs=P(("ctx", "tp"), None), check_vma=False
    )
```

```python
import jax
import jax.numpy as jnp
from jax import lax
from jax.experimental import pallas as pl
from jax.experimental.pallas import tpu as pltpu
from jax.sharding import PartitionSpec as P

HEAD_DIM = 128
BLOCK = 128
LINKS = 16
REACH = 4
GROUP = 4
HALF = BLOCK // 2
ROWS = GROUP * BLOCK
NEG = -1e30
RATE = 1.4426950408889634 * HEAD_DIM ** (-0.5)


SWAP = [(t, t ^ 1) for t in range(8)]


def swap(x):
    return lax.ppermute(x, "tp", SWAP)


def across_y(x, mask):
    return lax.ppermute(x, "tp", [(t, t ^ (2 * mask)) for t in range(8)])


def exchange(x, first):
    route = []
    for c in range(first, lax.axis_size("ctx") - 1, 2):
        route += [(c, c + 1), (c + 1, c)]
    return lax.ppermute(x, "ctx", route)


def smem():
    return pl.BlockSpec(memory_space=pltpu.SMEM)


def vmem():
    return pl.BlockSpec(memory_space=pltpu.VMEM)


def limit(mib):
    return pltpu.CompilerParams(vmem_limit_bytes=mib << 20)


def chip_and_core():
    t = lax.axis_index("tp")
    return t // 2, t % 2


def destination(which):
    chip, core = chip_and_core()
    return chip ^ (2, 1, 3, 0)[which], core


def project_kernel(*refs, counts, weights, added, finish, chips):
    refs = list(refs)
    xs = []
    for c in counts:
        xs.append([refs.pop(0) for _ in range(c)])
    ws = [refs.pop(0) for _ in range(weights)]
    before = [refs.pop(0) for _ in range(weights)] if added else [None] * weights
    chip, core = chip_and_core()
    accs = [None if ref is None else ref[...] for ref in before]
    for n, parts in enumerate(xs):
        x = parts[0][...] if len(parts) == 1 else jnp.concatenate([p[...] for p in parts], axis=0)
        width = x.shape[1]
        source = 2 * (chip ^ chips[n // 2]) + (core if n % 2 == 0 else 1 - core)
        first = pl.multiple_of(source * width, width)
        for k, w in enumerate(ws):
            part = jnp.dot(x, w[pl.ds(first, width), :], preferred_element_type=jnp.float32)
            accs[k] = part if accs[k] is None else accs[k] + part
    finish(refs, accs)


def project(chips, chunks, ws, before, out_shape, finish):
    flat = [part for chunk in chunks for part in chunk]
    counts = [len(chunk) for chunk in chunks]
    rows = sum(part.shape[0] for part in chunks[0])
    width = chunks[0][0].shape[1]
    cols = sum(w.shape[1] for w in ws)
    n = len(chunks)
    body = lambda *refs: project_kernel(
        *refs, counts=counts, weights=len(ws), added=bool(before), finish=finish, chips=chips
    )
    return pl.pallas_call(
        body,
        out_shape=out_shape,
        in_specs=[vmem()] * (len(flat) + len(ws) + len(before)),
        out_specs=jax.tree.map(lambda _: vmem(), out_shape),
        cost_estimate=pl.CostEstimate(
            flops=2 * rows * width * n * cols,
            transcendentals=0,
            bytes_accessed=2 * n * width * (rows + cols),
        ),
        compiler_params=limit(20),
    )(*flat, *ws, *before)


def half_of(x, second):
    rows = x.shape[0] // 2

    def body(x, out):
        out[...] = x[pl.ds(rows if second else 0, rows), :]

    return pl.pallas_call(
        body,
        out_shape=jax.ShapeDtypeStruct((rows, x.shape[1]), x.dtype),
        in_specs=[vmem()],
        out_specs=vmem(),
        compiler_params=limit(2),
    )(x)


def load_kernel(*refs):
    n = len(refs) // 2
    sems = refs[-1]
    copies = [pltpu.make_async_copy(refs[k], refs[n + k], sems.at[k]) for k in range(n)]
    for copy in copies:
        copy.start()
    for copy in copies:
        copy.wait()


def load(*arrays):
    return pl.pallas_call(
        load_kernel,
        out_shape=tuple(jax.ShapeDtypeStruct(x.shape, x.dtype) for x in arrays),
        in_specs=[pl.BlockSpec(memory_space=pltpu.HBM)] * len(arrays),
        out_specs=(vmem(),) * len(arrays),
        scratch_shapes=[pltpu.SemaphoreType.DMA((len(arrays),))],
        compiler_params=limit(12),
        name="load",
    )(*arrays)


def add_kernel(*refs):
    total = refs[0][...].astype(jnp.float32)
    for ref in refs[1:-1]:
        total = total + ref[...].astype(jnp.float32)
    refs[-1][...] = total.astype(jnp.bfloat16)


def add(*parts):
    return pl.pallas_call(
        add_kernel,
        out_shape=jax.ShapeDtypeStruct(parts[0].shape, parts[0].dtype),
        in_specs=[vmem()] * len(parts),
        out_specs=vmem(),
        compiler_params=limit(6),
        name="add",
    )(*parts)


def halves_kernel(a, b, low, high):
    rows = low.shape[0]
    total = a[...].astype(jnp.float32) + b[...].astype(jnp.float32)
    low[...] = total[:rows].astype(jnp.bfloat16)
    high[...] = total[rows:].astype(jnp.bfloat16)


def add_to_halves(a, b):
    shape = jax.ShapeDtypeStruct((a.shape[0] // 2, a.shape[1]), a.dtype)
    return pl.pallas_call(
        halves_kernel,
        out_shape=(shape, shape),
        in_specs=[vmem()] * 2,
        out_specs=(vmem(), vmem()),
        compiler_params=limit(6),
        name="add_to_halves",
    )(a, b)


def add_half(a, b, half, second):
    rows = half.shape[0]

    def body(a, b, half, out):
        total = a[...].astype(jnp.float32) + b[...].astype(jnp.float32)
        more = half[...].astype(jnp.float32)
        low, high = total[:rows], total[rows:]
        low, high = (low, high + more) if second else (low + more, high)
        out[pl.ds(0, rows), :] = low.astype(jnp.bfloat16)
        out[pl.ds(rows, rows), :] = high.astype(jnp.bfloat16)

    return pl.pallas_call(
        body,
        out_shape=jax.ShapeDtypeStruct(a.shape, a.dtype),
        in_specs=[vmem()] * 3,
        out_specs=vmem(),
        compiler_params=limit(6),
        name="add_half",
    )(a, b, half)


def keep_sums(out, accs):
    for ref, acc in zip(out, accs):
        ref[...] = acc


def store_kv(out, accs):
    kv = out[0]
    for b in range(kv.shape[1]):
        rows = slice(b * BLOCK, (b + 1) * BLOCK)
        kv[0, b] = accs[0][rows].T.astype(jnp.bfloat16)
        kv[1, b] = accs[1][rows].astype(jnp.bfloat16)


def store_q(out, accs):
    q = accs[0].astype(jnp.bfloat16)
    for b in range(q.shape[0] // BLOCK):
        for g in range(GROUP):
            out[0][b, pl.ds(g * BLOCK, BLOCK), :] = q[
                b * BLOCK : (b + 1) * BLOCK, g * HEAD_DIM : (g + 1) * HEAD_DIM
            ]


def absorb(table, line, q, below, above, m, l, acc):
    n = table[line, 0]

    def pick(kind, entry):
        return jnp.where(entry >= 4, above[kind, entry % 4], below[kind, entry % 4])

    def pair(p, carry):
        a = table[line, 1 + 2 * p]
        d = table[line, 2 + 2 * p]
        keys = jnp.concatenate([pick(0, a), pick(0, d)], axis=1)
        s = jnp.dot(q[...], keys, preferred_element_type=jnp.float32)
        s1 = s[:, :BLOCK]
        s2 = jnp.where(2 * p + 1 < n, s[:, BLOCK:], NEG)
        old = m[...]
        new = jnp.maximum(old, jnp.max(jnp.maximum(s1, s2), axis=1, keepdims=True))
        m[...] = new
        fade = jnp.exp2((old - new) * RATE)
        p1 = jnp.exp2((s1 - new) * RATE)
        p2 = jnp.exp2((s2 - new) * RATE)
        l[...] = l[...] * fade + (p1 + p2)
        w = jnp.concatenate([p1.astype(jnp.bfloat16), p2.astype(jnp.bfloat16)], axis=1)
        values = jnp.concatenate([pick(1, a), pick(1, d)], axis=0)
        acc[...] = acc[...] * fade + jnp.dot(w, values, preferred_element_type=jnp.float32)
        return carry

    lax.fori_loop(0, (n + 1) // 2, pair, 0)


def table_kernel(links, counts, docs, table):
    ctx = lax.axis_index("ctx")
    for line in range(5 * 4):
        table[line, 0] = 0
    for b in range(4):
        i = ctx * 4 + b
        mine = docs[i]
        live = counts[b]
        for s in range(1, LINKS):
            j = links[b, s]
            away = j // 4 - ctx
            line = jnp.abs(away) * 4 + b
            at = table[line, 0]
            ok = (s < live) & ((j < i) | (docs[j] != mine))
            table[line, 1 + at] = jnp.where((away > 0) == (ctx % 2 == 1), 4, 0) + j % 4
            table[line, 0] = at + ok.astype(jnp.int32)
    for line in range(5 * 4):
        table[line, 1 + table[line, 0]] = 0


def list_slots(links, counts, docs):
    return pl.pallas_call(
        table_kernel,
        out_shape=jax.ShapeDtypeStruct((5 * 4, LINKS + 2), jnp.int32),
        in_specs=[smem()] * 3,
        out_specs=smem(),
        compiler_params=limit(1),
        name="list_slots",
    )(links, counts, docs)


def begin(q, own, b, m, l, acc):
    s = jnp.dot(q[...], own[0, b], preferred_element_type=jnp.float32)
    row = lax.broadcasted_iota(jnp.int32, s.shape, 0) % BLOCK
    col = lax.broadcasted_iota(jnp.int32, s.shape, 1)
    s = jnp.where(col <= row, s, NEG)
    top = jnp.broadcast_to(jnp.max(s, axis=1, keepdims=True), s.shape)
    w = jnp.exp2((s - top) * RATE)
    m[...] = top
    l[...] = w
    acc[...] = jnp.dot(w.astype(jnp.bfloat16), own[1, b], preferred_element_type=jnp.float32)


def close(core, l, acc, wo, keep, give, wide):
    total = jnp.sum(l[...], axis=1, keepdims=True)
    res = (acc[...] / total).astype(jnp.bfloat16)
    for g in range(GROUP):
        wide[:, pl.ds(g * HEAD_DIM, HEAD_DIM)] = res[g * BLOCK : (g + 1) * BLOCK]
    mine = wide[pl.ds(pl.multiple_of(core * HALF, HALF), HALF), :]
    other = wide[pl.ds(pl.multiple_of((1 - core) * HALF, HALF), HALF), :]
    both = jnp.concatenate([mine, other], axis=0)
    term = jnp.dot(both, wo[...], preferred_element_type=jnp.float32).astype(jnp.bfloat16)
    keep[...] = term[:HALF]
    give[...] = term[HALF:]


def attend_kernel(table, q, *refs, which, steps, starts, ends):
    refs = list(refs)
    b, core = destination(which)
    q = q.at[b]
    own = refs.pop(0) if 0 in steps else None
    pieces = {k: (refs.pop(0), refs.pop(0)) for k in steps if k}
    state0 = [] if starts else [refs.pop(0) for _ in range(3)]
    wo = refs.pop(0) if ends else None
    if ends:
        keep, give, m, l, acc, wide = refs
    else:
        m, l, acc = refs
    if starts:
        begin(q, own, b, m, l, acc)
    else:
        for now, past in zip((m, l, acc), state0):
            now[...] = past[...]
    for k in steps:
        below, above = pieces[k] if k else (own, own)
        absorb(table, 4 * k + b, q, below, above, m, l, acc)
    if ends:
        close(core, l, acc, wo, keep, give, wide)


def attend(table, q, which, pieces, state, wo):
    steps = sorted(pieces)
    flat = [piece for k in steps for piece in pieces[k]]
    starts, ends = state is None, wo is not None
    one = jax.ShapeDtypeStruct((ROWS, HEAD_DIM), jnp.float32)
    scratch = [pltpu.VMEM((ROWS, HEAD_DIM), jnp.float32)] * 3
    if ends:
        out_shape = (jax.ShapeDtypeStruct((HALF, wo.shape[1]), jnp.bfloat16),) * 2
        scratch = scratch + [pltpu.VMEM((BLOCK, GROUP * HEAD_DIM), jnp.bfloat16)]
    else:
        out_shape, scratch = (one,) * 3, []
    args = flat + ([] if starts else list(state)) + ([wo] if ends else [])
    return pl.pallas_call(
        lambda *refs: attend_kernel(
            *refs, which=which, steps=steps, starts=starts, ends=ends
        ),
        out_shape=out_shape,
        in_specs=[smem()] + [vmem()] * (1 + len(args)),
        out_specs=(vmem(),) * len(out_shape),
        scratch_shapes=scratch,
        cost_estimate=pl.CostEstimate(
            flops=1 << 29, transcendentals=1 << 20, bytes_accessed=4 << 20
        ),
        compiler_params=limit(16),
    )(table, q, *args)


def layer(tokens, query_weight, key_weight, value_weight, out_weight, links, counts, doc_ids):
    rows = tokens.shape[0]
    table = list_slots(links, counts, doc_ids)

    up, down = across_y(tokens, 1), across_y(tokens, 3)
    twin = swap(tokens)
    key_weight, value_weight, query_weight, mine = load(key_weight, value_weight, query_weight, tokens)
    far_up = across_y(half_of(down, True), 1)
    far_down = across_y(half_of(up, False), 3)
    far = [far_down, far_up]
    first = [[mine], [twin], [up], [swap(up)], [down], [swap(down)]]
    second = [far, [swap(far_down), swap(far_up)]]

    sums = lambda *cols: tuple(jax.ShapeDtypeStruct((rows, n), jnp.float32) for n in cols)
    kv_weights = [key_weight, value_weight]
    *kv_sums, q_sums = project(
        (0, 1, 3), first, kv_weights + [query_weight], [], sums(128, 128, 512), keep_sums
    )
    kv_shape = (jax.ShapeDtypeStruct((2, rows // BLOCK, BLOCK, HEAD_DIM), jnp.bfloat16),)
    kv = project((2,), second, kv_weights, kv_sums, kv_shape, store_kv)[0]
    q_shape = (jax.ShapeDtypeStruct((rows // BLOCK, ROWS, HEAD_DIM), jnp.bfloat16),)
    q = project((2,), second, [query_weight], [q_sums], q_shape, store_q)[0]

    pieces = {0: (kv,)}
    even = odd = kv
    for k in range(1, REACH + 1):
        even, odd = exchange(odd, 0), exchange(even, 1)
        pieces[k] = even, odd

    def in_parts(which, cuts):
        state, start = None, 0
        for cut in cuts:
            part = {k: pieces[k] for k in range(start, cut)}
            wo = out_weight if cut > REACH else None
            state, start = attend(table, q, which, part, state, wo), cut
        return state

    keep, give = in_parts(0, (3, 4, 5))
    low, high = add_to_halves(keep, swap(give))
    low, high = across_y(low, 1), across_y(high, 3)
    keep, give = in_parts(1, (2, 4, 5))
    one = across_y(add_half(keep, swap(give), high, True), 1)
    keep, give = in_parts(2, (2, 4, 5))
    other = across_y(add_half(keep, swap(give), low, False), 3)
    keep, give = attend(table, q, 3, pieces, None, out_weight)
    return add(keep, swap(give), one, other)


def solution(mesh):
    placed = (
        P("ctx", "tp"),
        P(None, "tp"),
        P(None, "tp"),
        P(None, "tp"),
        P("tp", None),
        P("ctx", None),
        P("ctx"),
        P(),
    )
    return jax.shard_map(
        layer, mesh=mesh, in_specs=placed, out_specs=P(("ctx", "tp"), None), check_vma=False
    )
```
